32 devices in a mesh: section: 8 (over z, x), sp: 4 (over y, core).
Axes of the slice: x: 2, y: 2, z: 4, core: 2. Of those that a mesh axis runs over, the one named last changes fastest.
Arguments:
- slots: bfloat16 [8, 64, 3072], P('section', 'sp'), may hold values from -6 to 6
- patch_of_slot: int32 [8], replicated, may hold values from 0 to 7, each once
- step_of_slot: int32 [8], replicated, may hold values from 0 to 26
- modulation: bfloat16 [8, 28, 3, 3072], P('section'), may hold values from -4 to 4
- w_qkv: bfloat16 [8, 3072, 3, 2048], P('section', None, None, 'sp'), may hold values from -0.109375 to 0.109375
- qk_scale: bfloat16 [8, 2, 128], P('section'), may hold values from 0.25 to 4
- w_mlp_in: bfloat16 [8, 3072, 6144], P('section', None, 'sp'), may hold values from -0.109375 to 0.109375
- w_attn_out: bfloat16 [8, 2048, 3072], P('section', 'sp'), may hold values from -0.125 to 0.125
- w_mlp_out: bfloat16 [8, 6144, 3072], P('section', 'sp'), may hold values from -0.078125 to 0.078125
- kv_cache: bfloat16 [8, 2, 512, 2048], P('section', None, None, 'sp'), may hold values from -130 to 130
Outputs:
- slots_out: bfloat16 [8, 64, 3072], P('section', 'sp')
- kv_cache_out: bfloat16 [8, 2, 512, 2048], P('section', None, None, 'sp')
The draws below stay inside these ranges and needn't reach their ends.
Inputs may be any that keep to these rules, and one draw needn't show every extreme that they name: `patch_of_slot`: each patch id names exactly one slot.
All inputs are finite; a program needn't handle non-finite values.
Results may differ from the reference program's by a relative error of at most 0.012.
The reference program's roundings to bfloat16 on the way count: a program that leaves them out, or rounds other values in their place, can miss the bound.
Values may be sent and summed in bfloat16 or wider, within the bound.
A program may use at most 128 MiB of HBM per device.

```python
import math
import jax
import jax.numpy as jnp
from jax import lax

D = 3072
HD = 128
HEADS = 16
FF = 6144
STEPS = 28
ROUNDS = 2
LAYERS = 8
PATCHES = 8
PATCH_ROWS = 64
TOKENS = 512


def draw_qk_scale(key, part):
    key_b = jax.random.fold_in(jax.random.fold_in(key, 7), 1)
    array_shape = (LAYERS, 2, HD)
    exponent = jax.random.uniform(key_b, array_shape, jnp.float32, -1.3863, 1.3863)
    gains = jnp.exp(exponent)
    return gains.astype(jnp.bfloat16)


def draw_kv_cache(key, part):
    key_a, key_b = jax.random.split(key, 2)
    array_shape = (LAYERS, TOKENS, HEADS * HD)
    keys = jnp.clip(1.5 * jax.random.normal(key_a, array_shape, jnp.float32), -9.0, 9.0)
    values = jnp.clip(jax.random.normal(key_b, array_shape, jnp.float32), -6.0, 6.0)
    return jnp.stack([keys, values], axis=1).astype(jnp.bfloat16)


def plant(drawn, own_key, least, top_value):
    longest = drawn.shape.index(max(drawn.shape))
    spots = []
    for shift in (0, 1):
        where = [jax.random.randint(jax.random.fold_in(own_key, axis), (), 0, length) for axis, length in enumerate(drawn.shape)]
        where[longest] = (where[longest] + shift) % drawn.shape[longest]
        spots.append(tuple(where))
    return drawn.at[spots[0]].set(least).at[spots[1]].set(top_value)


def shard_levels(stream_key, extent, cuts, low, high):
    loudness, own = 1.0, jax.random.fold_in(stream_key, 6)
    for dim, blocks in cuts:
        draws = jnp.exp(jax.random.uniform(jax.random.fold_in(own, dim), (blocks,), jnp.float32, low / len(cuts), high / len(cuts)))
        loudness = loudness * jnp.repeat(draws, extent[dim] // blocks).reshape([-1 if axis == dim else 1 for axis in range(len(extent))])
    return loudness


def normal_values(key, extent, scale, reach, pieces=(), held_as=jnp.bfloat16):
    array = scale * jax.random.normal(key, extent, jnp.float32)
    if pieces:
        array = array * shard_levels(key, extent, pieces, -0.22, 0.18)
    return jnp.clip(array, -reach, reach).astype(held_as)


def setup_inputs(seed: int = 0) -> dict:
    streams_of = jax.random.split(jax.random.key(seed), 11)
    return {
        "slots": normal_values(streams_of[0], (PATCHES, PATCH_ROWS, D), 1.0, 6.0, ((0, 8), (1, 4))),
        "patch_of_slot": jax.random.permutation(streams_of[1], PATCHES).astype(jnp.int32),
        "step_of_slot": plant(jax.random.randint(streams_of[2], (PATCHES,), 0, STEPS - 1), jax.random.fold_in(streams_of[2], 1), 0, (STEPS - 1) - 1).astype(jnp.int32),
        "modulation": normal_values(streams_of[3], (LAYERS, STEPS, 3, D), 0.6, 4.0, ((0, 8),)),
        "w_qkv": normal_values(streams_of[4], (LAYERS, D, 3, HEADS * HD), D ** -0.5, 0.109375, ((0, 8), (3, 4))),
        "qk_scale": draw_qk_scale(jax.random.fold_in(streams_of[10], 71), 0),
        "w_mlp_in": normal_values(streams_of[6], (LAYERS, D, FF), D ** -0.5, 0.109375, ((0, 8), (2, 4))),
        "w_attn_out": normal_values(streams_of[7], (LAYERS, HEADS * HD, D), (HEADS * HD) ** -0.5, 0.125, ((0, 8), (1, 4))),
        "w_mlp_out": normal_values(streams_of[8], (LAYERS, FF, D), FF ** -0.5, 0.078125, ((0, 8), (1, 4))),
        "kv_cache": draw_kv_cache(jax.random.fold_in(streams_of[10], 71), 0),
    }


def head_norm(part, gain):
    rows = part.shape[0]
    wide = part.astype(jnp.float32).reshape(rows, -1, HD)
    power = lax.optimization_barrier(jnp.mean(wide * wide, axis=-1, keepdims=True))
    normed = wide * lax.rsqrt(power + 1e-06) * gain.astype(jnp.float32)
    return normed.astype(jnp.bfloat16).reshape(rows, -1)

def one_block(operands):
    slot, patch_id, timestep, table, qkv_weight, norm_gain, inner_weight, attention_weight, outer_weight, cache = operands
    factors = lax.dynamic_index_in_dim(table, timestep, 0, keepdims=False).astype(jnp.float32)
    wide = slot.astype(jnp.float32)
    center = wide - lax.optimization_barrier(jnp.mean(wide, axis=-1, keepdims=True))
    spread = lax.optimization_barrier(jnp.mean(center * center, axis=-1, keepdims=True))
    normed = (center * lax.rsqrt(spread + 1e-06) * (1.0 + factors[1]) + factors[0]).astype(jnp.bfloat16)
    projected = jnp.einsum('rd,dce->rce', normed.astype(jnp.float32), qkv_weight.astype(jnp.float32)).astype(jnp.bfloat16)
    query_normed = head_norm(projected[:, 0], norm_gain[0])
    key_normed = head_norm(projected[:, 1], norm_gain[1])
    first_row = (patch_id * PATCH_ROWS).astype(jnp.int32)
    keys = lax.dynamic_update_slice_in_dim(cache[0], key_normed, first_row, 0)
    values = lax.dynamic_update_slice_in_dim(cache[1], projected[:, 2], first_row, 0)
    queries = query_normed.astype(jnp.float32).reshape(PATCH_ROWS, HEADS, HD)
    key_heads = keys.astype(jnp.float32).reshape(TOKENS, HEADS, HD)
    value_heads = values.astype(jnp.float32).reshape(TOKENS, HEADS, HD)
    scores = jnp.einsum('rhd,thd->hrt', queries, key_heads) / math.sqrt(HD)
    shifted = jnp.exp(scores - lax.optimization_barrier(jnp.max(scores, axis=-1, keepdims=True)))
    weights = (shifted / lax.optimization_barrier(jnp.sum(shifted, axis=-1, keepdims=True))).astype(jnp.bfloat16)
    attention = jnp.einsum('hrt,thd->rhd', weights.astype(jnp.float32), value_heads).astype(jnp.bfloat16)
    attention = attention.reshape(PATCH_ROWS, HEADS * HD)
    activity = jax.nn.gelu(jnp.dot(normed, inner_weight, preferred_element_type=jnp.float32), approximate=True).astype(jnp.bfloat16)
    branch = jnp.dot(attention, attention_weight, preferred_element_type=jnp.float32) + jnp.dot(activity, outer_weight, preferred_element_type=jnp.float32)
    result = (wide + factors[2] * branch).astype(jnp.bfloat16)
    return (result, jnp.stack([keys, values]))

def reference(slots, patch_of_slot, step_of_slot, modulation, w_qkv, qk_scale, w_mlp_in, w_attn_out, w_mlp_out, kv_cache):
    current = slots
    cache = kv_cache
    patch_ids = patch_of_slot
    timesteps = step_of_slot
    first_slot = (jnp.arange(PATCHES) == 0).astype(jnp.int32)
    for round_id in range(ROUNDS):
        current, cache = lax.map(one_block, (current, patch_ids, timesteps, modulation, w_qkv, qk_scale, w_mlp_in, w_attn_out, w_mlp_out, cache))
        current = jnp.roll(current, 1, axis=0)
        patch_ids = jnp.roll(patch_ids, 1)
        timesteps = jnp.roll(timesteps, 1) + first_slot
    return (current, cache)
```

```python
import functools
import math

import jax
import jax.numpy as jnp
from jax import lax
from jax.experimental import pallas as pl
from jax.experimental.pallas import tpu as pltpu
from jax.sharding import PartitionSpec as P

HD = 128
ROUNDS = 2
CORES = 2
F32 = jnp.float32
BF16 = jnp.bfloat16
MESH = pl.DeviceIdType.MESH


def divides(total, wanted):
    return max(size for size in range(128, wanted + 1, 128) if total % size == 0)


def padded(rows):
    return max(rows, 128)


def kernel(sections, chips, patch_ref, step_ref, slots_hbm, mod_hbm, gain_hbm,
           qkv_hbm, inner_hbm, attn_hbm, outer_hbm, kv_hbm,
           x_out, kv_out,
           qkv, inner, attn_w, outer, kv, mod, gain,
           gathered, mine, core_part, core_land, chip_part, chip_land, fresh,
           h_buf, a_buf, act_buf, k_new, v_new, factors,
           load_sem, own_sem,
           ag_send, ag_recv, core_send, core_recv, chip_send, chip_recv, next_send, next_recv,
           relay_send, relay_recv):
    rows, width = fresh.shape[1:]
    half = chips * rows
    total_rows = CORES * half
    heads = qkv.shape[2] // HD
    hidden = inner.shape[1]
    tokens = kv.shape[1]
    blocks = tokens // total_rows
    chunks = core_send.shape[1]
    cut = width // chunks
    in_cut = divides(hidden, 512)
    in_chunks = hidden // in_cut
    me = lax.axis_index("sp")
    sid = lax.axis_index("section")
    chip = me // CORES
    core = lax.rem(me, CORES)
    partner = chip * CORES + (1 - core)
    following = lax.rem(sid + 1, sections)
    previous = lax.rem(sid + sections - 1, sections)

    def at_chip(k):
        return lax.rem(chip + k, chips) * CORES + core

    barrier = pltpu.get_barrier_semaphore()
    greeted = [{"sp": partner}] + [{"sp": at_chip(k)} for k in range(1, chips)]
    for k in range(chips):
        for other in (following, previous):
            greeted.append({"section": other, "sp": at_chip(k)})
    for device in greeted:
        pl.semaphore_signal(barrier, inc=1, device_id=device, device_id_type=MESH)

    loads = []

    def load(source, target):
        copy = pltpu.make_async_copy(source, target, load_sem.at[len(loads)])
        loads.append(copy)
        copy.start()
        return copy

    mod_load = load(mod_hbm, mod)
    gain_load = load(gain_hbm, gain)
    own_load = pltpu.make_async_copy(slots_hbm, gathered.at[0, 0, 0], own_sem)
    own_load.start()
    qkv_loads = [load(qkv_hbm.at[i], qkv.at[i]) for i in range(3)]

    pl.semaphore_wait(barrier, len(greeted))

    sends = []

    def send(source, target, send_sem, recv_sem, device):
        copy = pltpu.make_async_remote_copy(
            src_ref=source, dst_ref=target, send_sem=send_sem, recv_sem=recv_sem,
            device_id=device, device_id_type=MESH)
        copy.start()
        sends.append(copy)
        return copy

    across = [
        send(slots_hbm, gathered.at[0, 0, chips - k], ag_send.at[0, k], ag_recv.at[0, k], {"sp": at_chip(k)})
        for k in range(1, chips)
    ]
    beside = [send(slots_hbm, gathered.at[0, 1, 0], ag_send.at[1, 0], ag_recv.at[1, 0], {"sp": partner})]

    kv_load = load(kv_hbm, kv)
    inner_loads = [
        load(inner_hbm.at[:, pl.ds(i * in_cut, in_cut)], inner.at[:, pl.ds(i * in_cut, in_cut)])
        for i in range(in_chunks)
    ]
    out_loads = []
    for c in range(chunks):
        span = pl.ds(c * cut, cut)
        out_loads.append(
            (load(attn_hbm.at[:, span], attn_w.at[:, span]),
             load(outer_hbm.at[:, span], outer.at[:, span]))
        )

    if padded(total_rows) > total_rows:
        for buf in (h_buf, a_buf, act_buf):
            spare = padded(total_rows) - total_rows
            buf[total_rows:, :] = jnp.zeros((spare, buf.shape[1]), BF16)

    patches = []
    mod_load.wait()
    for r in range(ROUNDS):
        anchor = sid - r
        wrapped = (anchor < 0).astype(jnp.int32)
        anchor = anchor + wrapped * sections
        patches.append(patch_ref[anchor])
        step = step_ref[anchor] + wrapped
        table_rows = lax.broadcasted_iota(jnp.int32, (mod.shape[1], width), 0)
        for i in range(3):
            picked = jnp.where(table_rows == step, mod[i].astype(F32), 0.0)
            factors[r, i : i + 1, :] = jnp.sum(picked, axis=0, keepdims=True)

    def modulate(r, side, k):
        wide = gathered[r, side, k].astype(F32)
        center = wide - jnp.mean(wide, axis=-1, keepdims=True)
        spread = jnp.mean(center * center, axis=-1, keepdims=True)
        start = side * half + k * rows
        h_buf[start : start + rows, :] = (
            center * lax.rsqrt(spread + 1e-06) * (1.0 + factors[r, 1:2, :]) + factors[r, 0:1, :]
        ).astype(BF16)

    def dot(left, right):
        return jnp.dot(left[...], right, preferred_element_type=F32)[:total_rows]

    def head_norm(value, which):
        one = value.astype(F32)
        power = jnp.mean(one * one, axis=-1, keepdims=True)
        return (one * lax.rsqrt(power + 1e-06) * gain[which : which + 1, :].astype(F32)).astype(BF16)

    for r in range(ROUNDS):
        patch = patches[r]
        if r == 0:
            own_load.wait()
            modulate(r, 0, 0)
            beside[0].wait_recv()
            modulate(r, 1, 0)
            for k in range(1, chips):
                across[chips - k - 1].wait_recv()
                beside.append(send(gathered.at[0, 0, k], gathered.at[0, 1, k],
                                   ag_send.at[1, k], ag_recv.at[1, k], {"sp": partner}))
            for k in range(1, chips):
                modulate(r, 0, k)
            for k in range(1, chips):
                beside[k].wait_recv()
                modulate(r, 1, k)
        else:
            relays = []
            for c in range(chunks):
                span = pl.ds(c * cut, cut)
                for k in range(chips):
                    moves[c][k].wait_recv()
                    where = (chips - k) % chips
                    relays.append(send(gathered.at[r, 0, where, :, span], gathered.at[r, 1, where, :, span],
                                       relay_send.at[r, c, k], relay_recv.at[r, c, k], {"sp": partner}))
            for k in range(chips):
                modulate(r, 0, k)
            for copy in relays:
                copy.wait_recv()
            for k in range(chips):
                modulate(r, 1, k)

        made = []
        for i in range(3):
            if r == 0:
                qkv_loads[i].wait()
            made.append(dot(h_buf, qkv[i]).astype(BF16))
        if r == 0:
            gain_load.wait()
            kv_load.wait()

        column_block = lax.broadcasted_iota(jnp.int32, (total_rows, tokens), 1) // total_rows
        stale = column_block == patch
        queries, keys, values = [], [], []
        for head in range(heads):
            lanes = slice(head * HD, (head + 1) * HD)
            queries.append(head_norm(made[0][:, lanes], 0))
            keys.append(head_norm(made[1][:, lanes], 1))
            values.append(made[2][:, lanes])

        def attend(head):
            lanes = slice(head * HD, (head + 1) * HD)
            over = (((1,), (1,)), ((), ()))
            old = lax.dot_general(queries[head], kv[0, :, lanes], over, preferred_element_type=F32)
            new = lax.dot_general(queries[head], keys[head], over, preferred_element_type=F32)
            old = jnp.where(stale, -1e30, old)
            top = jnp.maximum(jnp.max(old, axis=-1, keepdims=True), jnp.max(new, axis=-1, keepdims=True))
            unit = math.log2(math.e) / math.sqrt(HD)
            old = jnp.exp2((old - top) * unit)
            new = jnp.exp2((new - top) * unit)
            scale = 1.0 / (jnp.sum(old, axis=-1, keepdims=True) + jnp.sum(new, axis=-1, keepdims=True))
            mixed = jnp.dot((old * scale).astype(BF16), kv[1, :, lanes], preferred_element_type=F32)
            mixed = mixed + jnp.dot((new * scale).astype(BF16), values[head], preferred_element_type=F32)
            a_buf[:total_rows, lanes] = mixed.astype(BF16)

        turns = max(heads, in_chunks)
        for turn in range(turns):
            if turn < heads:
                attend(turn)
            if turn < in_chunks:
                if r == 0:
                    inner_loads[turn].wait()
                span = slice(turn * in_cut, (turn + 1) * in_cut)
                act_buf[:total_rows, span] = jax.nn.gelu(dot(h_buf, inner[:, span]), approximate=True).astype(BF16)

        pairs, trades, moves = [], [], []

        def project(c):
            lanes = slice(c * cut, (c + 1) * cut)
            span = pl.ds(c * cut, cut)
            if r == 0:
                out_loads[c][0].wait()
                out_loads[c][1].wait()
            share = dot(act_buf, outer[:, lanes]) + dot(a_buf, attn_w[:, lanes])
            core_part[r, :, lanes] = share[half:].astype(BF16)
            pairs.append(send(core_part.at[r, :, span], core_land.at[r, :, span],
                              core_send.at[r, c], core_recv.at[r, c], {"sp": partner}))
            mine[:, lanes] = share[:half]

        def trade(c):
            lanes = slice(c * cut, (c + 1) * cut)
            span = pl.ds(c * cut, cut)
            pairs[c].wait_recv()
            both = mine[:, lanes] + core_land[r, :, lanes].astype(F32)
            mine[:rows, lanes] = both[:rows]
            group = []
            for k in range(1, chips):
                chip_part[r, k, :, lanes] = both[k * rows : (k + 1) * rows].astype(BF16)
                group.append(send(chip_part.at[r, k, :, span], chip_land.at[r, chips - k, :, span],
                                  chip_send.at[r, c, k], chip_recv.at[r, c, k], {"sp": at_chip(k)}))
            trades.append(group)

        def finish(c):
            lanes = slice(c * cut, (c + 1) * cut)
            span = pl.ds(c * cut, cut)
            for copy in trades[c]:
                copy.wait_recv()
            summed = mine[:rows, lanes]
            for k in range(1, chips):
                summed = summed + chip_land[r, k, :, lanes].astype(F32)
            fresh[r, :, lanes] = (
                gathered[r, 0, 0, :, lanes].astype(F32) + factors[r, 2:3, lanes] * summed
            ).astype(BF16)
            group = []
            if r < ROUNDS - 1:
                for k in range(chips):
                    group.append(send(fresh.at[r, :, span], gathered.at[r + 1, 0, (chips - k) % chips, :, span],
                                      next_send.at[r, c, k], next_recv.at[r, c, k],
                                      {"section": following, "sp": at_chip(k)}))
            else:
                group.append(send(fresh.at[r, :, span], x_out.at[:, span],
                                  next_send.at[r, c, 0], next_recv.at[r, c, 0], {"section": following}))
            moves.append(group)

        for c in range(chunks):
            project(c)
            if c > 0:
                trade(c - 1)
        trade(chunks - 1)

        for side in range(CORES):
            for k in range(chips):
                owner = lax.rem(chip + k, chips) * CORES + (core if side == 0 else 1 - core)
                there = pl.ds(pl.multiple_of(owner * rows, rows), rows)
                here = slice(side * half + k * rows, side * half + (k + 1) * rows)
                for head in range(heads):
                    lanes = slice(head * HD, (head + 1) * HD)
                    k_new[there, lanes] = keys[head][here]
                v_new[there, :] = made[2][here]
        target = kv if r < ROUNDS - 1 else kv_out
        for which, new in ((0, k_new), (1, v_new)):
            for p in range(blocks):
                there = slice(p * total_rows, (p + 1) * total_rows)
                hit = jnp.broadcast_to(patch, new.shape) == p
                target[which, there, :] = jnp.where(
                    hit, new[...].astype(F32), kv[which, there, :].astype(F32)).astype(BF16)

        for c in range(chunks):
            finish(c)

    for group in moves:
        for copy in group:
            copy.wait_recv()
    for copy in sends:
        copy.wait_send()


def shards(sections, peers, slots, patch_of_slot, step_of_slot, modulation, w_qkv, qk_scale,
           w_mlp_in, w_attn_out, w_mlp_out, kv_cache):
    rows, width = slots.shape[1:]
    local = w_qkv.shape[3]
    hidden = w_mlp_in.shape[2]
    chips = peers // CORES
    half = chips * rows
    total_rows = peers * rows
    chunks = width // divides(width, 768)
    loads = 2 + 3 + 1 + hidden // divides(hidden, 512) + 2 * chunks
    dma = pltpu.SemaphoreType.DMA
    vmem = pl.BlockSpec(memory_space=pltpu.VMEM)
    smem = pl.BlockSpec(memory_space=pltpu.SMEM)
    anywhere = pl.BlockSpec(memory_space=pl.ANY)
    x, kv = pl.pallas_call(
        functools.partial(kernel, sections, chips),
        out_shape=(
            pltpu.VMEM((rows, width), BF16),
            pltpu.VMEM(kv_cache.shape[1:], BF16),
        ),
        in_specs=[smem, smem] + [anywhere] * 8,
        out_specs=(vmem, vmem),
        scratch_shapes=[
            pltpu.VMEM((3, width, local), BF16),
            pltpu.VMEM((width, hidden), BF16),
            pltpu.VMEM((local, width), BF16),
            pltpu.VMEM((hidden, width), BF16),
            pltpu.VMEM(kv_cache.shape[1:], BF16),
            pltpu.VMEM((3, modulation.shape[1], width), BF16),
            pltpu.VMEM(qk_scale.shape[1:], BF16),
            pltpu.VMEM((ROUNDS, CORES, chips, rows, width), BF16),
            pltpu.VMEM((half, width), F32),
            pltpu.VMEM((ROUNDS, half, width), BF16),
            pltpu.VMEM((ROUNDS, half, width), BF16),
            pltpu.VMEM((ROUNDS, chips, rows, width), BF16),
            pltpu.VMEM((ROUNDS, chips, rows, width), BF16),
            pltpu.VMEM((ROUNDS, rows, width), BF16),
            pltpu.VMEM((padded(total_rows), width), BF16),
            pltpu.VMEM((padded(total_rows), local), BF16),
            pltpu.VMEM((padded(total_rows), hidden), BF16),
            pltpu.VMEM((total_rows, local), BF16),
            pltpu.VMEM((total_rows, local), BF16),
            pltpu.VMEM((ROUNDS, 8, width), F32),
            dma((loads,)),
            dma,
            dma((CORES, chips)),
            dma((CORES, chips)),
            dma((ROUNDS, chunks)),
            dma((ROUNDS, chunks)),
            dma((ROUNDS, chunks, chips)),
            dma((ROUNDS, chunks, chips)),
            dma((ROUNDS, chunks, chips)),
            dma((ROUNDS, chunks, chips)),
            dma((ROUNDS, chunks, chips)),
            dma((ROUNDS, chunks, chips)),
        ],
        compiler_params=pltpu.CompilerParams(
            collective_id=0, has_side_effects=True, vmem_limit_bytes=60 * 1024 * 1024
        ),
    )(
        patch_of_slot, step_of_slot, slots[0], jnp.transpose(modulation[0], (1, 0, 2)), qk_scale[0],
        jnp.transpose(w_qkv[0], (1, 0, 2)), w_mlp_in[0], w_attn_out[0], w_mlp_out[0], kv_cache[0],
    )
    return (x[None], kv[None])


def solution(mesh):
    return jax.shard_map(
        functools.partial(shards, mesh.shape["section"], mesh.shape["sp"]),
        mesh=mesh,
        in_specs=(
            P("section", "sp", None),
            P(),
            P(),
            P("section", None, None, None),
            P("section", None, None, "sp"),
            P("section", None, None),
            P("section", None, "sp"),
            P("section", "sp", None),
            P("section", "sp", None),
            P("section", None, None, "sp"),
        ),
        out_specs=(P("section", "sp", None), P("section", None, None, "sp")),
        check_vma=False,
    )
```

```python
import functools
import math

import jax
import jax.numpy as jnp
from jax import lax
from jax.experimental import pallas as pl
from jax.experimental.pallas import tpu as pltpu
from jax.sharding import PartitionSpec as P

HD = 128
ROUNDS = 2
CORES = 2
F32 = jnp.float32
BF16 = jnp.bfloat16
MESH = pl.DeviceIdType.MESH


def divides(total, wanted):
    return max(size for size in range(128, wanted + 1, 128) if total % size == 0)


def padded(rows):
    return max(rows, 128)


def kernel(sections, chips, patch_ref, step_ref, slots_hbm, mod_hbm, gain_hbm,
           qkv_hbm, inner_hbm, attn_hbm, outer_hbm, kv_hbm,
           x_out, kv_out,
           qkv, inner, attn_w, outer, kv, mod, gain,
           gathered, mine, core_part, core_land, chip_part, chip_land, fresh,
           h_buf, a_buf, act_buf, k_new, v_new, factors,
           load_sem, own_sem,
           ag_send, ag_recv, core_send, core_recv, chip_send, chip_recv, next_send, next_recv,
           relay_send, relay_recv):
    rows, width = fresh.shape[1:]
    half = chips * rows
    total_rows = CORES * half
    heads = qkv.shape[2] // HD
    hidden = inner.shape[1]
    tokens = kv.shape[1]
    blocks = tokens // total_rows
    chunks = core_send.shape[1]
    cut = width // chunks
    in_cut = divides(hidden, 512)
    in_chunks = hidden // in_cut
    me = lax.axis_index("sp")
    sid = lax.axis_index("section")
    chip = me // CORES
    core = lax.rem(me, CORES)
    partner = chip * CORES + (1 - core)
    following = lax.rem(sid + 1, sections)
    previous = lax.rem(sid + sections - 1, sections)

    def at_chip(k):
        return lax.rem(chip + k, chips) * CORES + core

    barrier = pltpu.get_barrier_semaphore()
    greeted = [{"section": previous, "sp": at_chip(k)} for k in range(chips)]
    greeted += [{"sp": at_chip(k)} for k in range(1, chips)] + [{"sp": partner}]
    for device in greeted:
        pl.semaphore_signal(barrier, inc=1, device_id=device, device_id_type=MESH)

    loads = []

    def load(source, target):
        copy = pltpu.make_async_copy(source, target, load_sem.at[len(loads)])
        loads.append(copy)
        copy.start()
        return copy

    mod_load = load(mod_hbm, mod)
    gain_load = load(gain_hbm, gain)
    own_load = pltpu.make_async_copy(slots_hbm, gathered.at[0, 0, 0], own_sem)
    own_load.start()
    qkv_loads = [load(qkv_hbm.at[i], qkv.at[i]) for i in range(3)]

    pl.semaphore_wait(barrier, len(greeted))

    sends = []

    def send(source, target, send_sem, recv_sem, device):
        copy = pltpu.make_async_remote_copy(
            src_ref=source, dst_ref=target, send_sem=send_sem, recv_sem=recv_sem,
            device_id=device, device_id_type=MESH)
        copy.start()
        sends.append(copy)
        return copy

    across = [
        send(slots_hbm, gathered.at[0, 0, chips - k], ag_send.at[0, k], ag_recv.at[0, k], {"sp": at_chip(k)})
        for k in range(1, chips)
    ]
    beside = [send(slots_hbm, gathered.at[0, 1, 0], ag_send.at[1, 0], ag_recv.at[1, 0], {"sp": partner})]

    kv_load = load(kv_hbm, kv)
    inner_loads = [
        load(inner_hbm.at[:, pl.ds(i * in_cut, in_cut)], inner.at[:, pl.ds(i * in_cut, in_cut)])
        for i in range(in_chunks)
    ]
    out_loads = []
    for c in range(chunks):
        span = pl.ds(c * cut, cut)
        out_loads.append(
            (load(attn_hbm.at[:, span], attn_w.at[:, span]),
             load(outer_hbm.at[:, span], outer.at[:, span]))
        )

    if padded(total_rows) > total_rows:
        for buf in (h_buf, a_buf, act_buf):
            spare = padded(total_rows) - total_rows
            buf[total_rows:, :] = jnp.zeros((spare, buf.shape[1]), BF16)

    patches = []
    mod_load.wait()
    for r in range(ROUNDS):
        anchor = sid - r
        wrapped = (anchor < 0).astype(jnp.int32)
        anchor = anchor + wrapped * sections
        patches.append(patch_ref[anchor])
        step = step_ref[anchor] + wrapped
        table_rows = lax.broadcasted_iota(jnp.int32, (mod.shape[1], width), 0)
        for i in range(3):
            picked = jnp.where(table_rows == step, mod[i].astype(F32), 0.0)
            factors[r, i : i + 1, :] = jnp.sum(picked, axis=0, keepdims=True)

    def modulate(r, side, k):
        wide = gathered[r, side, k].astype(F32)
        center = wide - jnp.mean(wide, axis=-1, keepdims=True)
        spread = jnp.mean(center * center, axis=-1, keepdims=True)
        start = side * half + k * rows
        h_buf[start : start + rows, :] = (
            center * lax.rsqrt(spread + 1e-06) * (1.0 + factors[r, 1:2, :]) + factors[r, 0:1, :]
        ).astype(BF16)

    def dot(left, right):
        return jnp.dot(left[...], right, preferred_element_type=F32)[:total_rows]

    def head_norm(value, which):
        one = value.astype(F32)
        power = jnp.mean(one * one, axis=-1, keepdims=True)
        return (one * lax.rsqrt(power + 1e-06) * gain[which : which + 1, :].astype(F32)).astype(BF16)

    for r in range(ROUNDS):
        patch = patches[r]
        if r == 0:
            own_load.wait()
            modulate(r, 0, 0)
            beside[0].wait_recv()
            modulate(r, 1, 0)
            for k in range(1, chips):
                across[chips - k - 1].wait_recv()
                beside.append(send(gathered.at[0, 0, k], gathered.at[0, 1, k],
                                   ag_send.at[1, k], ag_recv.at[1, k], {"sp": partner}))
            for k in range(1, chips):
                modulate(r, 0, k)
            for k in range(1, chips):
                beside[k].wait_recv()
                modulate(r, 1, k)
        else:
            relays = []
            for c in range(chunks):
                span = pl.ds(c * cut, cut)
                for k in range(chips):
                    moves[c][k].wait_recv()
                    where = (chips - k) % chips
                    relays.append(send(gathered.at[r, 0, where, :, span], gathered.at[r, 1, where, :, span],
                                       relay_send.at[r, c, k], relay_recv.at[r, c, k], {"sp": partner}))
            for k in range(chips):
                modulate(r, 0, k)
            for copy in relays:
                copy.wait_recv()
            for k in range(chips):
                modulate(r, 1, k)

        made = []
        for i in range(3):
            if r == 0:
                qkv_loads[i].wait()
            made.append(dot(h_buf, qkv[i]).astype(BF16))
        if r == 0:
            gain_load.wait()
            kv_load.wait()

        column_block = lax.broadcasted_iota(jnp.int32, (total_rows, tokens), 1) // total_rows
        stale = column_block == patch
        queries, keys, values = [], [], []
        for head in range(heads):
            lanes = slice(head * HD, (head + 1) * HD)
            queries.append(head_norm(made[0][:, lanes], 0))
            keys.append(head_norm(made[1][:, lanes], 1))
            values.append(made[2][:, lanes])

        over = (((1,), (1,)), ((), ()))
        unit = math.log2(math.e) / math.sqrt(HD)
        scored, weights = {}, {}

        def score(head):
            lanes = slice(head * HD, (head + 1) * HD)
            old = lax.dot_general(queries[head], kv[0, :, lanes], over, preferred_element_type=F32)
            new = lax.dot_general(queries[head], keys[head], over, preferred_element_type=F32)
            scored[head] = (jnp.where(stale, -1e30, old), new)

        def soften(head):
            old, new = scored[head]
            top = jnp.maximum(jnp.max(old, axis=-1, keepdims=True), jnp.max(new, axis=-1, keepdims=True))
            old = jnp.exp2((old - top) * unit)
            new = jnp.exp2((new - top) * unit)
            scale = 1.0 / (jnp.sum(old, axis=-1, keepdims=True) + jnp.sum(new, axis=-1, keepdims=True))
            weights[head] = ((old * scale).astype(BF16), (new * scale).astype(BF16))

        def mix(head):
            lanes = slice(head * HD, (head + 1) * HD)
            old, new = weights[head]
            mixed = jnp.dot(old, kv[1, :, lanes], preferred_element_type=F32)
            mixed = mixed + jnp.dot(new, values[head], preferred_element_type=F32)
            a_buf[:total_rows, lanes] = mixed.astype(BF16)

        for head in range(heads):
            score(head)
        for turn in range(in_chunks):
            if r == 0:
                inner_loads[turn].wait()
            span = slice(turn * in_cut, (turn + 1) * in_cut)
            act_buf[:total_rows, span] = jax.nn.gelu(dot(h_buf, inner[:, span]), approximate=True).astype(BF16)
            shared = -(-heads // max(in_chunks - 1, 1))
            for head in range(turn * shared, min((turn + 1) * shared, heads)):
                soften(head)
        for head in range(heads):
            mix(head)

        pairs, trades, moves = [], [], []

        def project(c):
            lanes = slice(c * cut, (c + 1) * cut)
            span = pl.ds(c * cut, cut)
            if r == 0:
                out_loads[c][0].wait()
                out_loads[c][1].wait()
            share = dot(act_buf, outer[:, lanes]) + dot(a_buf, attn_w[:, lanes])
            core_part[r, :, lanes] = share[half:].astype(BF16)
            pairs.append(send(core_part.at[r, :, span], core_land.at[r, :, span],
                              core_send.at[r, c], core_recv.at[r, c], {"sp": partner}))
            mine[:, lanes] = share[:half]

        def trade(c):
            lanes = slice(c * cut, (c + 1) * cut)
            span = pl.ds(c * cut, cut)
            pairs[c].wait_recv()
            both = mine[:, lanes] + core_land[r, :, lanes].astype(F32)
            group = []
            if r == ROUNDS - 1:
                for k in range(chips):
                    term = factors[r, 2:3, lanes] * both[k * rows : (k + 1) * rows]
                    if k == 0:
                        term = term + gathered[r, 0, 0, :, lanes].astype(F32)
                    chip_part[r, k, :, lanes] = term.astype(BF16)
                    group.append(send(chip_part.at[r, k, :, span], chip_land.at[r, (chips - k) % chips, :, span],
                                      chip_send.at[r, c, k], chip_recv.at[r, c, k],
                                      {"section": following, "sp": at_chip(k)}))
                trades.append(group)
                return
            mine[:rows, lanes] = both[:rows]
            for k in range(1, chips):
                chip_part[r, k, :, lanes] = both[k * rows : (k + 1) * rows].astype(BF16)
                group.append(send(chip_part.at[r, k, :, span], chip_land.at[r, chips - k, :, span],
                                  chip_send.at[r, c, k], chip_recv.at[r, c, k], {"sp": at_chip(k)}))
            trades.append(group)

        def finish(c):
            lanes = slice(c * cut, (c + 1) * cut)
            span = pl.ds(c * cut, cut)
            for copy in trades[c]:
                copy.wait_recv()
            if r == ROUNDS - 1:
                summed = chip_land[r, 0, :, lanes].astype(F32)
                for k in range(1, chips):
                    summed = summed + chip_land[r, k, :, lanes].astype(F32)
                x_out[:, lanes] = summed.astype(BF16)
                return
            summed = mine[:rows, lanes]
            for k in range(1, chips):
                summed = summed + chip_land[r, k, :, lanes].astype(F32)
            fresh[r, :, lanes] = (
                gathered[r, 0, 0, :, lanes].astype(F32) + factors[r, 2:3, lanes] * summed
            ).astype(BF16)
            group = []
            for k in range(chips):
                group.append(send(fresh.at[r, :, span], gathered.at[r + 1, 0, (chips - k) % chips, :, span],
                                  next_send.at[r, c, k], next_recv.at[r, c, k],
                                  {"section": following, "sp": at_chip(k)}))
            moves.append(group)

        for c in range(chunks + 2):
            if c < chunks:
                project(c)
            if c > 1:
                trade(c - 2)

        for side in range(CORES):
            for k in range(chips):
                owner = lax.rem(chip + k, chips) * CORES + (core if side == 0 else 1 - core)
                there = pl.ds(pl.multiple_of(owner * rows, rows), rows)
                here = slice(side * half + k * rows, side * half + (k + 1) * rows)
                for head in range(heads):
                    lanes = slice(head * HD, (head + 1) * HD)
                    k_new[there, lanes] = keys[head][here]
                v_new[there, :] = made[2][here]
        target = kv if r < ROUNDS - 1 else kv_out
        for which, new in ((0, k_new), (1, v_new)):
            for p in range(blocks):
                there = slice(p * total_rows, (p + 1) * total_rows)
                hit = jnp.broadcast_to(patch, new.shape) == p
                target[which, there, :] = jnp.where(
                    hit, new[...].astype(F32), kv[which, there, :].astype(F32)).astype(BF16)

        for c in range(chunks):
            finish(c)

    for copy in sends:
        copy.wait_send()


def shards(sections, peers, slots, patch_of_slot, step_of_slot, modulation, w_qkv, qk_scale,
           w_mlp_in, w_attn_out, w_mlp_out, kv_cache):
    rows, width = slots.shape[1:]
    local = w_qkv.shape[3]
    hidden = w_mlp_in.shape[2]
    chips = peers // CORES
    half = chips * rows
    total_rows = peers * rows
    chunks = width // divides(width, 768)
    loads = 2 + 3 + 1 + hidden // divides(hidden, 512) + 2 * chunks
    dma = pltpu.SemaphoreType.DMA
    vmem = pl.BlockSpec(memory_space=pltpu.VMEM)
    smem = pl.BlockSpec(memory_space=pltpu.SMEM)
    anywhere = pl.BlockSpec(memory_space=pl.ANY)
    x, kv = pl.pallas_call(
        functools.partial(kernel, sections, chips),
        out_shape=(
            pltpu.VMEM((rows, width), BF16),
            pltpu.VMEM(kv_cache.shape[1:], BF16),
        ),
        in_specs=[smem, smem] + [anywhere] * 8,
        out_specs=(vmem, vmem),
        scratch_shapes=[
            pltpu.VMEM((3, width, local), BF16),
            pltpu.VMEM((width, hidden), BF16),
            pltpu.VMEM((local, width), BF16),
            pltpu.VMEM((hidden, width), BF16),
            pltpu.VMEM(kv_cache.shape[1:], BF16),
            pltpu.VMEM((3, modulation.shape[1], width), BF16),
            pltpu.VMEM(qk_scale.shape[1:], BF16),
            pltpu.VMEM((ROUNDS, CORES, chips, rows, width), BF16),
            pltpu.VMEM((half, width), F32),
            pltpu.VMEM((ROUNDS, half, width), BF16),
            pltpu.VMEM((ROUNDS, half, width), BF16),
            pltpu.VMEM((ROUNDS, chips, rows, width), BF16),
            pltpu.VMEM((ROUNDS, chips, rows, width), BF16),
            pltpu.VMEM((ROUNDS, rows, width), BF16),
            pltpu.VMEM((padded(total_rows), width), BF16),
            pltpu.VMEM((padded(total_rows), local), BF16),
            pltpu.VMEM((padded(total_rows), hidden), BF16),
            pltpu.VMEM((total_rows, local), BF16),
            pltpu.VMEM((total_rows, local), BF16),
            pltpu.VMEM((ROUNDS, 8, width), F32),
            dma((loads,)),
            dma,
            dma((CORES, chips)),
            dma((CORES, chips)),
            dma((ROUNDS, chunks)),
            dma((ROUNDS, chunks)),
            dma((ROUNDS, chunks, chips)),
            dma((ROUNDS, chunks, chips)),
            dma((ROUNDS, chunks, chips)),
            dma((ROUNDS, chunks, chips)),
            dma((ROUNDS, chunks, chips)),
            dma((ROUNDS, chunks, chips)),
        ],
        compiler_params=pltpu.CompilerParams(
            collective_id=0, has_side_effects=True, vmem_limit_bytes=60 * 1024 * 1024
        ),
    )(
        patch_of_slot, step_of_slot, slots[0], jnp.transpose(modulation[0], (1, 0, 2)), qk_scale[0],
        jnp.transpose(w_qkv[0], (1, 0, 2)), w_mlp_in[0], w_attn_out[0], w_mlp_out[0], kv_cache[0],
    )
    return (x[None], kv[None])


def solution(mesh):
    return jax.shard_map(
        functools.partial(shards, mesh.shape["section"], mesh.shape["sp"]),
        mesh=mesh,
        in_specs=(
            P("section", "sp", None),
            P(),
            P(),
            P("section", None, None, None),
            P("section", None, None, "sp"),
            P("section", None, None),
            P("section", None, "sp"),
            P("section", "sp", None),
            P("section", "sp", None),
            P("section", None, None, "sp"),
        ),
        out_specs=(P("section", "sp", None), P("section", None, None, "sp")),
        check_vma=False,
    )
```

```python
import functools
import math

import jax
import jax.numpy as jnp
from jax import lax
from jax.experimental import pallas as pl
from jax.experimental.pallas import tpu as pltpu
from jax.sharding import PartitionSpec as P

HD = 128
ROUNDS = 2
CORES = 2
F32 = jnp.float32
BF16 = jnp.bfloat16
MESH = pl.DeviceIdType.MESH


def divides(total, wanted):
    return max(size for size in range(128, wanted + 1, 128) if total % size == 0)


def padded(rows):
    return max(rows, 128)


def kernel(sections, chips, patch_hbm, step_hbm, slots_hbm, mod_hbm, gain_hbm,
           qkv_hbm, inner_hbm, attn_hbm, outer_hbm, kv_hbm,
           x_out, kv_out,
           qkv, inner, attn_w, outer, kv, mod, gain,
           gathered, mine, core_part, core_land, chip_part, chip_land, fresh,
           h_buf, a_buf, act_buf, k_new, v_new, factors,
           patch_ref, step_ref, load_sem, own_sem, plan_sem,
           ag_send, ag_recv, core_send, core_recv, chip_send, chip_recv, next_send, next_recv,
           relay_send, relay_recv):
    rows, width = x_out.shape
    half = chips * rows
    total_rows = CORES * half
    heads = qkv.shape[2] // HD
    hidden = inner.shape[1]
    tokens = kv.shape[1]
    blocks = tokens // total_rows
    chunks = core_send.shape[1]
    cut = width // chunks
    in_cut = divides(hidden, 512)
    in_chunks = hidden // in_cut
    me = lax.axis_index("sp")
    sid = lax.axis_index("section")
    chip = me // CORES
    core = lax.rem(me, CORES)
    partner = chip * CORES + (1 - core)
    following = lax.rem(sid + 1, sections)
    previous = lax.rem(sid + sections - 1, sections)

    def at_chip(k):
        return lax.rem(chip + k, chips) * CORES + core

    barrier = pltpu.get_barrier_semaphore()
    greeted = [{"section": previous, "sp": at_chip(k)} for k in range(chips)]
    greeted += [{"sp": at_chip(k)} for k in range(1, chips)] + [{"sp": partner}]
    for device in greeted:
        pl.semaphore_signal(barrier, inc=1, device_id=device, device_id_type=MESH)

    loads = []

    def load(source, target):
        copy = pltpu.make_async_copy(source, target, load_sem.at[len(loads)])
        loads.append(copy)
        copy.start()
        return copy

    plan_loads = [pltpu.make_async_copy(patch_hbm, patch_ref, plan_sem.at[0]),
                  pltpu.make_async_copy(step_hbm, step_ref, plan_sem.at[1])]
    for copy in plan_loads:
        copy.start()
    mod_load = load(mod_hbm, mod)
    gain_load = load(gain_hbm, gain)
    own_load = pltpu.make_async_copy(slots_hbm, gathered.at[0, 0, 0], own_sem)
    own_load.start()
    qkv_loads = [load(qkv_hbm.at[i], qkv.at[i]) for i in range(3)]

    pl.semaphore_wait(barrier, len(greeted))

    sends = []

    def send(source, target, send_sem, recv_sem, device):
        copy = pltpu.make_async_remote_copy(
            src_ref=source, dst_ref=target, send_sem=send_sem, recv_sem=recv_sem,
            device_id=device, device_id_type=MESH)
        copy.start()
        sends.append(copy)
        return copy

    across = [
        send(slots_hbm, gathered.at[0, 0, chips - k], ag_send.at[0, k], ag_recv.at[0, k], {"sp": at_chip(k)})
        for k in range(1, chips)
    ]
    beside = [send(slots_hbm, gathered.at[0, 1, 0], ag_send.at[1, 0], ag_recv.at[1, 0], {"sp": partner})]

    kv_load = load(kv_hbm, kv)
    inner_loads = [
        load(inner_hbm.at[:, pl.ds(i * in_cut, in_cut)], inner.at[:, pl.ds(i * in_cut, in_cut)])
        for i in range(in_chunks)
    ]
    out_loads = []

    if padded(total_rows) > total_rows:
        for buf in (h_buf, a_buf, act_buf):
            spare = padded(total_rows) - total_rows
            buf[total_rows:, :] = jnp.zeros((spare, buf.shape[1]), BF16)

    patches = []
    mod_load.wait()
    for copy in plan_loads:
        copy.wait()
    for r in range(ROUNDS):
        anchor = sid - r
        wrapped = (anchor < 0).astype(jnp.int32)
        anchor = anchor + wrapped * sections
        patches.append(patch_ref[anchor])
        step = step_ref[anchor] + wrapped
        table_rows = lax.broadcasted_iota(jnp.int32, (mod.shape[1], width), 0)
        for i in range(3):
            picked = jnp.where(table_rows == step, mod[i].astype(F32), 0.0)
            factors[r, i : i + 1, :] = jnp.sum(picked, axis=0, keepdims=True)

    def modulate(r, side, k):
        wide = gathered[r, side, k].astype(F32)
        center = wide - jnp.mean(wide, axis=-1, keepdims=True)
        spread = jnp.mean(center * center, axis=-1, keepdims=True)
        start = side * half + k * rows
        h_buf[start : start + rows, :] = (
            center * lax.rsqrt(spread + 1e-06) * (1.0 + factors[r, 1:2, :]) + factors[r, 0:1, :]
        ).astype(BF16)

    def dot(left, right):
        return jnp.dot(left[...], right, preferred_element_type=F32)[:total_rows]

    def head_norm(value, which):
        one = value.astype(F32)
        power = jnp.mean(one * one, axis=-1, keepdims=True)
        return (one * lax.rsqrt(power + 1e-06) * gain[which : which + 1, :].astype(F32)).astype(BF16)

    for r in range(ROUNDS):
        patch = patches[r]
        if r == 0:
            own_load.wait()
            modulate(r, 0, 0)
            beside[0].wait_recv()
            modulate(r, 1, 0)
            for k in range(1, chips):
                across[chips - k - 1].wait_recv()
                beside.append(send(gathered.at[0, 0, k], gathered.at[0, 1, k],
                                   ag_send.at[1, k], ag_recv.at[1, k], {"sp": partner}))
            for c in range(chunks):
                span = pl.ds(c * cut, cut)
                out_loads.append(
                    (load(attn_hbm.at[:, span], attn_w.at[:, span]),
                     load(outer_hbm.at[:, span], outer.at[:, span]))
                )
            for k in range(1, chips):
                modulate(r, 0, k)
            for k in range(1, chips):
                beside[k].wait_recv()
                modulate(r, 1, k)
        else:
            relays = []
            for c in range(chunks):
                span = pl.ds(c * cut, cut)
                for k in range(chips):
                    moves[c][k].wait_recv()
                    where = (chips - k) % chips
                    relays.append(send(gathered.at[r, 0, where, :, span], gathered.at[r, 1, where, :, span],
                                       relay_send.at[r, c, k], relay_recv.at[r, c, k], {"sp": partner}))
            for k in range(chips):
                modulate(r, 0, k)
            for copy in relays:
                copy.wait_recv()
            for k in range(chips):
                modulate(r, 1, k)

        made = []
        for i in range(3):
            if r == 0:
                qkv_loads[i].wait()
            made.append(dot(h_buf, qkv[i]).astype(BF16))
        if r == 0:
            gain_load.wait()
            kv_load.wait()

        column_block = lax.broadcasted_iota(jnp.int32, (total_rows, tokens), 1) // total_rows
        stale = column_block == patch
        queries, keys, values = [], [], []
        for head in range(heads):
            lanes = slice(head * HD, (head + 1) * HD)
            queries.append(head_norm(made[0][:, lanes], 0))
            keys.append(head_norm(made[1][:, lanes], 1))
            values.append(made[2][:, lanes])

        over = (((1,), (1,)), ((), ()))
        unit = math.log2(math.e) / math.sqrt(HD)
        scored, weights = {}, {}

        def score(head):
            lanes = slice(head * HD, (head + 1) * HD)
            old = lax.dot_general(queries[head], kv[0, :, lanes], over, preferred_element_type=F32)
            new = lax.dot_general(queries[head], keys[head], over, preferred_element_type=F32)
            scored[head] = (jnp.where(stale, -1e30, old), new)

        def soften(head):
            old, new = scored[head]
            top = jnp.maximum(jnp.max(old, axis=-1, keepdims=True), jnp.max(new, axis=-1, keepdims=True))
            old = jnp.exp2((old - top) * unit)
            new = jnp.exp2((new - top) * unit)
            scale = 1.0 / (jnp.sum(old, axis=-1, keepdims=True) + jnp.sum(new, axis=-1, keepdims=True))
            weights[head] = ((old * scale).astype(BF16), (new * scale).astype(BF16))

        def mix(head):
            lanes = slice(head * HD, (head + 1) * HD)
            old, new = weights[head]
            mixed = jnp.dot(old, kv[1, :, lanes], preferred_element_type=F32)
            mixed = mixed + jnp.dot(new, values[head], preferred_element_type=F32)
            a_buf[:total_rows, lanes] = mixed.astype(BF16)

        for head in range(heads):
            score(head)
        for turn in range(in_chunks):
            if r == 0:
                inner_loads[turn].wait()
            span = slice(turn * in_cut, (turn + 1) * in_cut)
            act_buf[:total_rows, span] = jax.nn.gelu(dot(h_buf, inner[:, span]), approximate=True).astype(BF16)
            shared = -(-heads // max(in_chunks - 1, 1))
            for head in range(turn * shared, min((turn + 1) * shared, heads)):
                soften(head)
        for head in range(heads):
            mix(head)

        pairs, trades, moves = [], [], []

        def project(c):
            lanes = slice(c * cut, (c + 1) * cut)
            if r == 0:
                out_loads[c][0].wait()
                out_loads[c][1].wait()
            return dot(act_buf, outer[:, lanes]) + dot(a_buf, attn_w[:, lanes])

        def keep(c, share):
            core_part[r, c] = share[half:].astype(BF16)
            mine[:, c * cut : (c + 1) * cut] = share[:half]

        def pair(c):
            pairs.append(send(core_part.at[r, c], core_land.at[r, c],
                              core_send.at[r, c], core_recv.at[r, c], {"sp": partner}))

        def trade(c):
            lanes = slice(c * cut, (c + 1) * cut)
            span = pl.ds(c * cut, cut)
            pairs[c].wait_recv()
            both = mine[:, lanes] + core_land[r, c].astype(F32)
            group = []
            if r == ROUNDS - 1:
                for k in range(chips):
                    term = factors[r, 2:3, lanes] * both[k * rows : (k + 1) * rows]
                    if k == 0:
                        term = term + gathered[r, 0, 0, :, lanes].astype(F32)
                    chip_part[r, c, k] = term.astype(BF16)
                    group.append(send(chip_part.at[r, c, k], chip_land.at[r, c, (chips - k) % chips],
                                      chip_send.at[r, c, k], chip_recv.at[r, c, k],
                                      {"section": following, "sp": at_chip(k)}))
                trades.append(group)
                return
            mine[:rows, lanes] = both[:rows]
            for k in range(1, chips):
                chip_part[r, c, k] = both[k * rows : (k + 1) * rows].astype(BF16)
                group.append(send(chip_part.at[r, c, k], chip_land.at[r, c, chips - k],
                                  chip_send.at[r, c, k], chip_recv.at[r, c, k], {"sp": at_chip(k)}))
            trades.append(group)

        def finish(c):
            lanes = slice(c * cut, (c + 1) * cut)
            span = pl.ds(c * cut, cut)
            for copy in trades[c]:
                copy.wait_recv()
            if r == ROUNDS - 1:
                summed = chip_land[r, c, 0].astype(F32)
                for k in range(1, chips):
                    summed = summed + chip_land[r, c, k].astype(F32)
                x_out[:, lanes] = summed.astype(BF16)
                return
            summed = mine[:rows, lanes]
            for k in range(1, chips):
                summed = summed + chip_land[r, c, k].astype(F32)
            fresh[r, c] = (
                gathered[r, 0, 0, :, lanes].astype(F32) + factors[r, 2:3, lanes] * summed
            ).astype(BF16)
            group = []
            for k in range(chips):
                group.append(send(fresh.at[r, c], gathered.at[r + 1, 0, (chips - k) % chips, :, span],
                                  next_send.at[r, c, k], next_recv.at[r, c, k],
                                  {"section": following, "sp": at_chip(k)}))
            moves.append(group)

        for c in range(chunks + 3):
            if c < chunks:
                share = project(c)
            if 0 < c <= chunks:
                pair(c - 1)
            if c > 2:
                trade(c - 3)
            if c < chunks:
                keep(c, share)

        if r < ROUNDS - 1:
            for c in range(chunks):
                finish(c)

        for side in range(CORES):
            for k in range(chips):
                owner = lax.rem(chip + k, chips) * CORES + (core if side == 0 else 1 - core)
                there = pl.ds(pl.multiple_of(owner * rows, rows), rows)
                here = slice(side * half + k * rows, side * half + (k + 1) * rows)
                for head in range(heads):
                    lanes = slice(head * HD, (head + 1) * HD)
                    k_new[there, lanes] = keys[head][here]
                v_new[there, :] = made[2][here]
        target = kv if r < ROUNDS - 1 else kv_out
        for which, new in ((0, k_new), (1, v_new)):
            for p in range(blocks):
                there = slice(p * total_rows, (p + 1) * total_rows)
                hit = jnp.broadcast_to(patch, new.shape) == p
                target[which, there, :] = jnp.where(
                    hit, new[...].astype(F32), kv[which, there, :].astype(F32)).astype(BF16)

        if r == ROUNDS - 1:
            for c in range(chunks):
                finish(c)

    for copy in sends:
        copy.wait_send()


def shards(sections, peers, slots, patch_of_slot, step_of_slot, modulation, w_qkv, qk_scale,
           w_mlp_in, w_attn_out, w_mlp_out, kv_cache):
    rows, width = slots.shape[1:]
    local = w_qkv.shape[3]
    hidden = w_mlp_in.shape[2]
    chips = peers // CORES
    half = chips * rows
    total_rows = peers * rows
    cut = divides(width, 512)
    chunks = width // cut
    loads = 2 + 3 + 1 + hidden // divides(hidden, 512) + 2 * chunks
    dma = pltpu.SemaphoreType.DMA
    vmem = pl.BlockSpec(memory_space=pltpu.VMEM)
    anywhere = pl.BlockSpec(memory_space=pl.ANY)
    x, kv = pl.pallas_call(
        functools.partial(kernel, sections, chips),
        out_shape=(
            pltpu.VMEM((rows, width), BF16),
            pltpu.VMEM(kv_cache.shape[1:], BF16),
        ),
        in_specs=[anywhere] * 10,
        out_specs=(vmem, vmem),
        scratch_shapes=[
            pltpu.VMEM((3, width, local), BF16),
            pltpu.VMEM((width, hidden), BF16),
            pltpu.VMEM((local, width), BF16),
            pltpu.VMEM((hidden, width), BF16),
            pltpu.VMEM(kv_cache.shape[1:], BF16),
            pltpu.VMEM((3, modulation.shape[1], width), BF16),
            pltpu.VMEM(qk_scale.shape[1:], BF16),
            pltpu.VMEM((ROUNDS, CORES, chips, rows, width), BF16),
            pltpu.VMEM((half, width), F32),
            pltpu.VMEM((ROUNDS, chunks, half, cut), BF16),
            pltpu.VMEM((ROUNDS, chunks, half, cut), BF16),
            pltpu.VMEM((ROUNDS, chunks, chips, rows, cut), BF16),
            pltpu.VMEM((ROUNDS, chunks, chips, rows, cut), BF16),
            pltpu.VMEM((ROUNDS, chunks, rows, cut), BF16),
            pltpu.VMEM((padded(total_rows), width), BF16),
            pltpu.VMEM((padded(total_rows), local), BF16),
            pltpu.VMEM((padded(total_rows), hidden), BF16),
            pltpu.VMEM((total_rows, local), BF16),
            pltpu.VMEM((total_rows, local), BF16),
            pltpu.VMEM((ROUNDS, 8, width), F32),
            pltpu.SMEM(patch_of_slot.shape, jnp.int32),
            pltpu.SMEM(step_of_slot.shape, jnp.int32),
            dma((loads,)),
            dma,
            dma((2,)),
            dma((CORES, chips)),
            dma((CORES, chips)),
            dma((ROUNDS, chunks)),
            dma((ROUNDS, chunks)),
            dma((ROUNDS, chunks, chips)),
            dma((ROUNDS, chunks, chips)),
            dma((ROUNDS, chunks, chips)),
            dma((ROUNDS, chunks, chips)),
            dma((ROUNDS, chunks, chips)),
            dma((ROUNDS, chunks, chips)),
        ],
        compiler_params=pltpu.CompilerParams(
            collective_id=0, has_side_effects=True, vmem_limit_bytes=60 * 1024 * 1024
        ),
    )(
        patch_of_slot, step_of_slot, slots[0], jnp.transpose(modulation[0], (1, 0, 2)), qk_scale[0],
        jnp.transpose(w_qkv[0], (1, 0, 2)), w_mlp_in[0], w_attn_out[0], w_mlp_out[0], kv_cache[0],
    )
    return (x[None], kv[None])


def solution(mesh):
    return jax.shard_map(
        functools.partial(shards, mesh.shape["section"], mesh.shape["sp"]),
        mesh=mesh,
        in_specs=(
            P("section", "sp", None),
            P(),
            P(),
            P("section", None, None, None),
            P("section", None, None, "sp"),
            P("section", None, None),
            P("section", None, "sp"),
            P("section", "sp", None),
            P("section", "sp", None),
            P("section", None, None, "sp"),
        ),
        out_specs=(P("section", "sp", None), P("section", None, None, "sp")),
        check_vma=False,
    )
```

```python
import functools
import math

import jax
import jax.numpy as jnp
from jax import lax
from jax.experimental import pallas as pl
from jax.experimental.pallas import tpu as pltpu
from jax.sharding import PartitionSpec as P

HD = 128
ROUNDS = 2
CORES = 2
F32 = jnp.float32
BF16 = jnp.bfloat16
MESH = pl.DeviceIdType.MESH


def divides(total, wanted):
    return max(size for size in range(128, wanted + 1, 128) if total % size == 0)


def padded(rows):
    return max(rows, 128)


def kernel(sections, chips, patch_hbm, step_hbm, slots_hbm, mod_hbm, gain_hbm,
           qkv_hbm, inner_hbm, attn_hbm, outer_hbm, kv_hbm,
           x_out, kv_out,
           qkv, inner, attn_w, outer, kv, mod, gain,
           gathered, mine, core_part, core_land, chip_part, chip_land, fresh,
           h_buf, a_buf, act_buf, k_new, v_new, factors,
           patch_ref, step_ref, load_sem, own_sem, plan_sem,
           ag_send, ag_recv, core_send, core_recv, chip_send, chip_recv, next_send, next_recv,
           relay_send, relay_recv):
    rows, width = x_out.shape
    half = chips * rows
    total_rows = CORES * half
    heads = qkv.shape[2] // HD
    hidden = inner.shape[1]
    tokens = kv.shape[1]
    blocks = tokens // total_rows
    chunks = core_send.shape[1]
    cut = width // chunks
    in_cut = divides(hidden, 512)
    in_chunks = hidden // in_cut
    me = lax.axis_index("sp")
    sid = lax.axis_index("section")
    chip = me // CORES
    core = lax.rem(me, CORES)
    partner = chip * CORES + (1 - core)
    following = lax.rem(sid + 1, sections)
    previous = lax.rem(sid + sections - 1, sections)

    def at_chip(k):
        return lax.rem(chip + k, chips) * CORES + core

    barrier = pltpu.get_barrier_semaphore()
    greeted = [{"section": previous, "sp": at_chip(k)} for k in range(chips)]
    greeted += [{"sp": at_chip(k)} for k in range(1, chips)] + [{"sp": partner}]
    for device in greeted:
        pl.semaphore_signal(barrier, inc=1, device_id=device, device_id_type=MESH)

    loads = []

    def load(source, target):
        copy = pltpu.make_async_copy(source, target, load_sem.at[len(loads)])
        loads.append(copy)
        copy.start()
        return copy

    plan_loads = [pltpu.make_async_copy(patch_hbm, patch_ref, plan_sem.at[0]),
                  pltpu.make_async_copy(step_hbm, step_ref, plan_sem.at[1])]
    for copy in plan_loads:
        copy.start()
    mod_load = load(mod_hbm, mod)
    gain_load = load(gain_hbm, gain)
    own_load = pltpu.make_async_copy(slots_hbm, gathered.at[0, 0, 0], own_sem)
    own_load.start()
    qkv_loads = [load(qkv_hbm.at[i], qkv.at[i]) for i in range(3)]

    pl.semaphore_wait(barrier, len(greeted))

    sends = []

    def send(source, target, send_sem, recv_sem, device):
        copy = pltpu.make_async_remote_copy(
            src_ref=source, dst_ref=target, send_sem=send_sem, recv_sem=recv_sem,
            device_id=device, device_id_type=MESH)
        copy.start()
        sends.append(copy)
        return copy

    across = [
        send(slots_hbm, gathered.at[0, 0, chips - k], ag_send.at[0, k], ag_recv.at[0, k], {"sp": at_chip(k)})
        for k in range(1, chips)
    ]
    beside = [send(slots_hbm, gathered.at[0, 1, 0], ag_send.at[1, 0], ag_recv.at[1, 0], {"sp": partner})]

    kv_load = load(kv_hbm, kv)
    inner_loads = [
        load(inner_hbm.at[:, pl.ds(i * in_cut, in_cut)], inner.at[:, pl.ds(i * in_cut, in_cut)])
        for i in range(in_chunks)
    ]
    out_loads = []

    if padded(total_rows) > total_rows:
        for buf in (h_buf, a_buf, act_buf):
            spare = padded(total_rows) - total_rows
            buf[total_rows:, :] = jnp.zeros((spare, buf.shape[1]), BF16)

    patches = []
    mod_load.wait()
    for copy in plan_loads:
        copy.wait()
    for r in range(ROUNDS):
        anchor = sid - r
        wrapped = (anchor < 0).astype(jnp.int32)
        anchor = anchor + wrapped * sections
        patches.append(patch_ref[anchor])
        step = step_ref[anchor] + wrapped
        table_rows = lax.broadcasted_iota(jnp.int32, (mod.shape[1], width), 0)
        for i in range(3):
            picked = jnp.where(table_rows == step, mod[i].astype(F32), 0.0)
            factors[r, i : i + 1, :] = jnp.sum(picked, axis=0, keepdims=True)

    def modulate(r, side, k):
        wide = gathered[r, side, k].astype(F32)
        center = wide - jnp.mean(wide, axis=-1, keepdims=True)
        spread = jnp.mean(center * center, axis=-1, keepdims=True)
        start = side * half + k * rows
        h_buf[start : start + rows, :] = (
            center * lax.rsqrt(spread + 1e-06) * (1.0 + factors[r, 1:2, :]) + factors[r, 0:1, :]
        ).astype(BF16)

    def dot(left, right):
        return jnp.dot(left[...], right, preferred_element_type=F32)[:total_rows]

    def head_norm(value, which):
        one = value.astype(F32)
        power = jnp.mean(one * one, axis=-1, keepdims=True)
        return (one * lax.rsqrt(power + 1e-06) * gain[which : which + 1, :].astype(F32)).astype(BF16)

    for r in range(ROUNDS):
        patch = patches[r]
        if r == 0:
            own_load.wait()
            modulate(r, 0, 0)
            beside[0].wait_recv()
            modulate(r, 1, 0)
            for k in range(1, chips):
                across[chips - k - 1].wait_recv()
                beside.append(send(gathered.at[0, 0, k], gathered.at[0, 1, k],
                                   ag_send.at[1, k], ag_recv.at[1, k], {"sp": partner}))
            for c in range(chunks):
                span = pl.ds(c * cut, cut)
                out_loads.append(
                    (load(attn_hbm.at[:, span], attn_w.at[:, span]),
                     load(outer_hbm.at[:, span], outer.at[:, span]))
                )
            for k in range(1, chips):
                modulate(r, 0, k)
            for k in range(1, chips):
                beside[k].wait_recv()
                modulate(r, 1, k)
        else:
            relays = []
            for c in range(chunks):
                span = pl.ds(c * cut, cut)
                for k in range(chips):
                    moves[c][k].wait_recv()
                    where = (chips - k) % chips
                    relays.append(send(gathered.at[r, 0, where, :, span], gathered.at[r, 1, where, :, span],
                                       relay_send.at[r, c, k], relay_recv.at[r, c, k], {"sp": partner}))
            for k in range(chips):
                modulate(r, 0, k)
            for copy in relays:
                copy.wait_recv()
            for k in range(chips):
                modulate(r, 1, k)

        made = []
        for i in range(3):
            if r == 0:
                qkv_loads[i].wait()
            made.append(dot(h_buf, qkv[i]).astype(BF16))
        if r == 0:
            gain_load.wait()
            kv_load.wait()

        column_block = lax.broadcasted_iota(jnp.int32, (total_rows, tokens), 1) // total_rows
        stale = column_block == patch
        queries, keys, values = [], [], []
        for head in range(heads):
            lanes = slice(head * HD, (head + 1) * HD)
            queries.append(head_norm(made[0][:, lanes], 0))
            keys.append(head_norm(made[1][:, lanes], 1))
            values.append(made[2][:, lanes])

        over = (((1,), (1,)), ((), ()))
        unit = math.log2(math.e) / math.sqrt(HD)
        scored, weights = {}, {}

        def score(head):
            lanes = slice(head * HD, (head + 1) * HD)
            old = lax.dot_general(queries[head], kv[0, :, lanes], over, preferred_element_type=F32)
            new = lax.dot_general(queries[head], keys[head], over, preferred_element_type=F32)
            scored[head] = (jnp.where(stale, -1e30, old), new)

        def soften(head):
            old, new = scored[head]
            top = jnp.maximum(jnp.max(old, axis=-1, keepdims=True), jnp.max(new, axis=-1, keepdims=True))
            old = jnp.exp2((old - top) * unit)
            new = jnp.exp2((new - top) * unit)
            scale = 1.0 / (jnp.sum(old, axis=-1, keepdims=True) + jnp.sum(new, axis=-1, keepdims=True))
            weights[head] = ((old * scale).astype(BF16), (new * scale).astype(BF16))

        def mix(head):
            lanes = slice(head * HD, (head + 1) * HD)
            old, new = weights[head]
            mixed = jnp.dot(old, kv[1, :, lanes], preferred_element_type=F32)
            mixed = mixed + jnp.dot(new, values[head], preferred_element_type=F32)
            a_buf[:total_rows, lanes] = mixed.astype(BF16)

        for head in range(heads):
            score(head)
        for turn in range(in_chunks):
            if r == 0:
                inner_loads[turn].wait()
            span = slice(turn * in_cut, (turn + 1) * in_cut)
            act_buf[:total_rows, span] = jax.nn.gelu(dot(h_buf, inner[:, span]), approximate=True).astype(BF16)
            shared = -(-heads // max(in_chunks - 1, 1))
            for head in range(turn * shared, min((turn + 1) * shared, heads)):
                soften(head)
        for head in range(heads):
            mix(head)

        pairs, trades, moves = [], [], []

        def project(c):
            lanes = slice(c * cut, (c + 1) * cut)
            if r == 0:
                out_loads[c][0].wait()
                out_loads[c][1].wait()
            return dot(act_buf, outer[:, lanes]) + dot(a_buf, attn_w[:, lanes])

        def keep(c, share):
            core_part[r, c] = share[half:].astype(BF16)
            mine[:, c * cut : (c + 1) * cut] = share[:half]

        def pair(c):
            pairs.append(send(core_part.at[r, c], core_land.at[r, c],
                              core_send.at[r, c], core_recv.at[r, c], {"sp": partner}))

        def straight(c):
            return r == ROUNDS - 1 and c >= chunks // 2

        def trade(c):
            lanes = slice(c * cut, (c + 1) * cut)
            span = pl.ds(c * cut, cut)
            pairs[c].wait_recv()
            both = mine[:, lanes] + core_land[r, c].astype(F32)
            group = []
            if straight(c):
                for k in reversed(range(chips)):
                    term = factors[r, 2:3, lanes] * both[k * rows : (k + 1) * rows]
                    if k == 0:
                        term = term + gathered[r, 0, 0, :, lanes].astype(F32)
                    chip_part[r, c, k] = term.astype(BF16)
                    group.append(send(chip_part.at[r, c, k], chip_land.at[r, c, (chips - k) % chips],
                                      chip_send.at[r, c, k], chip_recv.at[r, c, k],
                                      {"section": following, "sp": at_chip(k)}))
                trades.append(group)
                return
            mine[:rows, lanes] = both[:rows]
            for k in range(1, chips):
                chip_part[r, c, k] = both[k * rows : (k + 1) * rows].astype(BF16)
                group.append(send(chip_part.at[r, c, k], chip_land.at[r, c, chips - k],
                                  chip_send.at[r, c, k], chip_recv.at[r, c, k], {"sp": at_chip(k)}))
            trades.append(group)

        def finish(c):
            lanes = slice(c * cut, (c + 1) * cut)
            span = pl.ds(c * cut, cut)
            for copy in trades[c]:
                copy.wait_recv()
            if straight(c):
                summed = chip_land[r, c, 0].astype(F32)
                for k in range(1, chips):
                    summed = summed + chip_land[r, c, k].astype(F32)
                x_out[:, lanes] = summed.astype(BF16)
                return
            summed = mine[:rows, lanes]
            for k in range(1, chips):
                summed = summed + chip_land[r, c, k].astype(F32)
            fresh[r, c] = (
                gathered[r, 0, 0, :, lanes].astype(F32) + factors[r, 2:3, lanes] * summed
            ).astype(BF16)
            group = []
            for k in reversed(range(chips if r < ROUNDS - 1 else 1)):
                target = x_out.at[:, span] if r == ROUNDS - 1 else gathered.at[r + 1, 0, (chips - k) % chips, :, span]
                group.append(send(fresh.at[r, c], target, next_send.at[r, c, k], next_recv.at[r, c, k],
                                  {"section": following, "sp": at_chip(k)}))
            moves.append(group[::-1])

        for c in range(chunks + 4):
            if c < chunks:
                share = project(c)
            if 0 < c <= chunks:
                pair(c - 1)
            if c > 3:
                trade(c - 4)
            if c < chunks:
                keep(c, share)

        if r < ROUNDS - 1:
            for c in range(chunks):
                finish(c)

        for side in range(CORES):
            for k in range(chips):
                owner = lax.rem(chip + k, chips) * CORES + (core if side == 0 else 1 - core)
                there = pl.ds(pl.multiple_of(owner * rows, rows), rows)
                here = slice(side * half + k * rows, side * half + (k + 1) * rows)
                for head in range(heads):
                    lanes = slice(head * HD, (head + 1) * HD)
                    k_new[there, lanes] = keys[head][here]
                v_new[there, :] = made[2][here]
        target = kv if r < ROUNDS - 1 else kv_out
        for which, new in ((0, k_new), (1, v_new)):
            for p in range(blocks):
                there = slice(p * total_rows, (p + 1) * total_rows)
                hit = jnp.broadcast_to(patch, new.shape) == p
                target[which, there, :] = jnp.where(
                    hit, new[...].astype(F32), kv[which, there, :].astype(F32)).astype(BF16)

        if r == ROUNDS - 1:
            for c in range(chunks):
                finish(c)

    for group in moves:
        for copy in group:
            copy.wait_recv()
    for copy in sends:
        copy.wait_send()


def shards(sections, peers, slots, patch_of_slot, step_of_slot, modulation, w_qkv, qk_scale,
           w_mlp_in, w_attn_out, w_mlp_out, kv_cache):
    rows, width = slots.shape[1:]
    local = w_qkv.shape[3]
    hidden = w_mlp_in.shape[2]
    chips = peers // CORES
    half = chips * rows
    total_rows = peers * rows
    cut = divides(width, 512)
    chunks = width // cut
    loads = 2 + 3 + 1 + hidden // divides(hidden, 512) + 2 * chunks
    dma = pltpu.SemaphoreType.DMA
    vmem = pl.BlockSpec(memory_space=pltpu.VMEM)
    anywhere = pl.BlockSpec(memory_space=pl.ANY)
    x, kv = pl.pallas_call(
        functools.partial(kernel, sections, chips),
        out_shape=(
            pltpu.VMEM((rows, width), BF16),
            pltpu.VMEM(kv_cache.shape[1:], BF16),
        ),
        in_specs=[anywhere] * 10,
        out_specs=(vmem, vmem),
        scratch_shapes=[
            pltpu.VMEM((3, width, local), BF16),
            pltpu.VMEM((width, hidden), BF16),
            pltpu.VMEM((local, width), BF16),
            pltpu.VMEM((hidden, width), BF16),
            pltpu.VMEM(kv_cache.shape[1:], BF16),
            pltpu.VMEM((3, modulation.shape[1], width), BF16),
            pltpu.VMEM(qk_scale.shape[1:], BF16),
            pltpu.VMEM((ROUNDS, CORES, chips, rows, width), BF16),
            pltpu.VMEM((half, width), F32),
            pltpu.VMEM((ROUNDS, chunks, half, cut), BF16),
            pltpu.VMEM((ROUNDS, chunks, half, cut), BF16),
            pltpu.VMEM((ROUNDS, chunks, chips, rows, cut), BF16),
            pltpu.VMEM((ROUNDS, chunks, chips, rows, cut), BF16),
            pltpu.VMEM((ROUNDS, chunks, rows, cut), BF16),
            pltpu.VMEM((padded(total_rows), width), BF16),
            pltpu.VMEM((padded(total_rows), local), BF16),
            pltpu.VMEM((padded(total_rows), hidden), BF16),
            pltpu.VMEM((total_rows, local), BF16),
            pltpu.VMEM((total_rows, local), BF16),
            pltpu.VMEM((ROUNDS, 8, width), F32),
            pltpu.SMEM(patch_of_slot.shape, jnp.int32),
            pltpu.SMEM(step_of_slot.shape, jnp.int32),
            dma((loads,)),
            dma,
            dma((2,)),
            dma((CORES, chips)),
            dma((CORES, chips)),
            dma((ROUNDS, chunks)),
            dma((ROUNDS, chunks)),
            dma((ROUNDS, chunks, chips)),
            dma((ROUNDS, chunks, chips)),
            dma((ROUNDS, chunks, chips)),
            dma((ROUNDS, chunks, chips)),
            dma((ROUNDS, chunks, chips)),
            dma((ROUNDS, chunks, chips)),
        ],
        compiler_params=pltpu.CompilerParams(
            collective_id=0, has_side_effects=True, vmem_limit_bytes=60 * 1024 * 1024
        ),
    )(
        patch_of_slot, step_of_slot, slots[0], jnp.transpose(modulation[0], (1, 0, 2)), qk_scale[0],
        jnp.transpose(w_qkv[0], (1, 0, 2)), w_mlp_in[0], w_attn_out[0], w_mlp_out[0], kv_cache[0],
    )
    return (x[None], kv[None])


def solution(mesh):
    return jax.shard_map(
        functools.partial(shards, mesh.shape["section"], mesh.shape["sp"]),
        mesh=mesh,
        in_specs=(
            P("section", "sp", None),
            P(),
            P(),
            P("section", None, None, None),
            P("section", None, None, "sp"),
            P("section", None, None),
            P("section", None, "sp"),
            P("section", "sp", None),
            P("section", "sp", None),
            P("section", None, None, "sp"),
        ),
        out_specs=(P("section", "sp", None), P("section", None, None, "sp")),
        check_vma=False,
    )
```

```python
import functools
import math

import jax
import jax.numpy as jnp
from jax import lax
from jax.experimental import pallas as pl
from jax.experimental.pallas import tpu as pltpu
from jax.sharding import PartitionSpec as P

HD = 128
ROUNDS = 2
CORES = 2
F32 = jnp.float32
BF16 = jnp.bfloat16
MESH = pl.DeviceIdType.MESH


def divides(total, wanted):
    return max(size for size in range(128, wanted + 1, 128) if total % size == 0)


def padded(rows):
    return max(rows, 128)


def kernel(sections, chips, patch_hbm, step_hbm, slots_hbm, mod_hbm, gain_hbm,
           qkv_hbm, inner_hbm, attn_hbm, outer_hbm, kv_hbm,
           x_out, kv_out,
           qkv, inner, attn_w, outer, kv, mod, gain,
           gathered, mine, core_part, core_land, chip_part, chip_land, fresh, far_part, far_land,
           h_buf, a_buf, act_buf, k_new, v_new, factors,
           patch_ref, step_ref, load_sem, own_sem, plan_sem,
           ag_send, ag_recv, core_send, core_recv, chip_send, chip_recv, next_send, next_recv,
           relay_send, relay_recv):
    rows, width = x_out.shape
    half = chips * rows
    total_rows = CORES * half
    heads = qkv.shape[2] // HD
    hidden = inner.shape[1]
    tokens = kv.shape[1]
    blocks = tokens // total_rows
    chunks = core_send.shape[1]
    cut = width // chunks
    in_cut = divides(hidden, 512)
    in_chunks = hidden // in_cut
    me = lax.axis_index("sp")
    sid = lax.axis_index("section")
    chip = me // CORES
    core = lax.rem(me, CORES)
    partner = chip * CORES + (1 - core)
    following = lax.rem(sid + 1, sections)
    previous = lax.rem(sid + sections - 1, sections)

    def at_chip(k):
        return lax.rem(chip + k, chips) * CORES + core

    barrier = pltpu.get_barrier_semaphore()
    greeted = [{"section": previous, "sp": at_chip(k)} for k in range(chips)]
    greeted += [{"sp": at_chip(k)} for k in range(1, chips)] + [{"sp": partner}]
    for device in greeted:
        pl.semaphore_signal(barrier, inc=1, device_id=device, device_id_type=MESH)

    loads = []

    def load(source, target):
        copy = pltpu.make_async_copy(source, target, load_sem.at[len(loads)])
        loads.append(copy)
        copy.start()
        return copy

    plan_loads = [pltpu.make_async_copy(patch_hbm, patch_ref, plan_sem.at[0]),
                  pltpu.make_async_copy(step_hbm, step_ref, plan_sem.at[1])]
    for copy in plan_loads:
        copy.start()
    mod_load = load(mod_hbm, mod)
    gain_load = load(gain_hbm, gain)
    own_load = pltpu.make_async_copy(slots_hbm, gathered.at[0, 0, 0], own_sem)
    own_load.start()
    qkv_loads = [load(qkv_hbm.at[i], qkv.at[i]) for i in range(3)]

    pl.semaphore_wait(barrier, len(greeted))

    sends = []

    def send(source, target, send_sem, recv_sem, device):
        copy = pltpu.make_async_remote_copy(
            src_ref=source, dst_ref=target, send_sem=send_sem, recv_sem=recv_sem,
            device_id=device, device_id_type=MESH)
        copy.start()
        sends.append(copy)
        return copy

    across = [
        send(slots_hbm, gathered.at[0, 0, chips - k], ag_send.at[0, k], ag_recv.at[0, k], {"sp": at_chip(k)})
        for k in range(1, chips)
    ]
    beside = [send(slots_hbm, gathered.at[0, 1, 0], ag_send.at[1, 0], ag_recv.at[1, 0], {"sp": partner})]

    kv_load = load(kv_hbm, kv)
    inner_loads = [
        load(inner_hbm.at[:, pl.ds(i * in_cut, in_cut)], inner.at[:, pl.ds(i * in_cut, in_cut)])
        for i in range(in_chunks)
    ]
    out_loads = []

    if padded(total_rows) > total_rows:
        for buf in (h_buf, a_buf, act_buf):
            spare = padded(total_rows) - total_rows
            buf[total_rows:, :] = jnp.zeros((spare, buf.shape[1]), BF16)

    patches = []
    mod_load.wait()
    for copy in plan_loads:
        copy.wait()
    for r in range(ROUNDS):
        anchor = sid - r
        wrapped = (anchor < 0).astype(jnp.int32)
        anchor = anchor + wrapped * sections
        patches.append(patch_ref[anchor])
        step = step_ref[anchor] + wrapped
        table_rows = lax.broadcasted_iota(jnp.int32, (mod.shape[1], width), 0)
        for i in range(3):
            picked = jnp.where(table_rows == step, mod[i].astype(F32), 0.0)
            factors[r, i : i + 1, :] = jnp.sum(picked, axis=0, keepdims=True)

    def modulate(r, side, k):
        wide = gathered[r, side, k].astype(F32)
        center = wide - jnp.mean(wide, axis=-1, keepdims=True)
        spread = jnp.mean(center * center, axis=-1, keepdims=True)
        start = side * half + k * rows
        h_buf[start : start + rows, :] = (
            center * lax.rsqrt(spread + 1e-06) * (1.0 + factors[r, 1:2, :]) + factors[r, 0:1, :]
        ).astype(BF16)

    def dot(left, right):
        return jnp.dot(left[...], right, preferred_element_type=F32)[:total_rows]

    def head_norm(value, which):
        one = value.astype(F32)
        power = jnp.mean(one * one, axis=-1, keepdims=True)
        return (one * lax.rsqrt(power + 1e-06) * gain[which : which + 1, :].astype(F32)).astype(BF16)

    for r in range(ROUNDS):
        patch = patches[r]
        if r == 0:
            own_load.wait()
            modulate(r, 0, 0)
            beside[0].wait_recv()
            modulate(r, 1, 0)
            for k in range(1, chips):
                across[chips - k - 1].wait_recv()
                beside.append(send(gathered.at[0, 0, k], gathered.at[0, 1, k],
                                   ag_send.at[1, k], ag_recv.at[1, k], {"sp": partner}))
            for c in range(chunks):
                span = pl.ds(c * cut, cut)
                out_loads.append(
                    (load(attn_hbm.at[:, span], attn_w.at[:, span]),
                     load(outer_hbm.at[:, span], outer.at[:, span]))
                )
            for k in range(1, chips):
                modulate(r, 0, k)
            for k in range(1, chips):
                beside[k].wait_recv()
                modulate(r, 1, k)
        else:
            relays = []
            for c in range(chunks):
                span = pl.ds(c * cut, cut)
                if moves[c] is None:
                    for copy in trades[c]:
                        copy.wait_recv()
                    for k in range(chips):
                        summed = far_land[r - 1, 0, k].astype(F32)
                        for m in range(1, chips):
                            summed = summed + far_land[r - 1, m, (k + chips - m) % chips].astype(F32)
                        gathered[r, 0, k, :, c * cut : (c + 1) * cut] = summed.astype(BF16)
                for k in range(chips):
                    if moves[c] is not None:
                        moves[c][k].wait_recv()
                    where = (chips - k) % chips
                    relays.append(send(gathered.at[r, 0, where, :, span], gathered.at[r, 1, where, :, span],
                                       relay_send.at[r, c, k], relay_recv.at[r, c, k], {"sp": partner}))
            for k in range(chips):
                modulate(r, 0, k)
            for copy in relays:
                copy.wait_recv()
            for k in range(chips):
                modulate(r, 1, k)

        made = []
        for i in range(3):
            if r == 0:
                qkv_loads[i].wait()
            made.append(dot(h_buf, qkv[i]).astype(BF16))
        if r == 0:
            gain_load.wait()
            kv_load.wait()

        column_block = lax.broadcasted_iota(jnp.int32, (total_rows, tokens), 1) // total_rows
        stale = column_block == patch
        queries, keys, values = [], [], []
        for head in range(heads):
            lanes = slice(head * HD, (head + 1) * HD)
            queries.append(head_norm(made[0][:, lanes], 0))
            keys.append(head_norm(made[1][:, lanes], 1))
            values.append(made[2][:, lanes])

        over = (((1,), (1,)), ((), ()))
        unit = math.log2(math.e) / math.sqrt(HD)
        scored, weights = {}, {}

        def score(head):
            lanes = slice(head * HD, (head + 1) * HD)
            old = lax.dot_general(queries[head], kv[0, :, lanes], over, preferred_element_type=F32)
            new = lax.dot_general(queries[head], keys[head], over, preferred_element_type=F32)
            scored[head] = (jnp.where(stale, -1e30, old), new)

        def soften(head):
            old, new = scored[head]
            top = jnp.maximum(jnp.max(old, axis=-1, keepdims=True), jnp.max(new, axis=-1, keepdims=True))
            old = jnp.exp2((old - top) * unit)
            new = jnp.exp2((new - top) * unit)
            scale = 1.0 / (jnp.sum(old, axis=-1, keepdims=True) + jnp.sum(new, axis=-1, keepdims=True))
            weights[head] = ((old * scale).astype(BF16), (new * scale).astype(BF16))

        def mix(head):
            lanes = slice(head * HD, (head + 1) * HD)
            old, new = weights[head]
            mixed = jnp.dot(old, kv[1, :, lanes], preferred_element_type=F32)
            mixed = mixed + jnp.dot(new, values[head], preferred_element_type=F32)
            a_buf[:total_rows, lanes] = mixed.astype(BF16)

        for head in range(heads):
            score(head)
        for turn in range(in_chunks):
            if r == 0:
                inner_loads[turn].wait()
            span = slice(turn * in_cut, (turn + 1) * in_cut)
            act_buf[:total_rows, span] = jax.nn.gelu(dot(h_buf, inner[:, span]), approximate=True).astype(BF16)
            shared = -(-heads // max(in_chunks - 1, 1))
            for head in range(turn * shared, min((turn + 1) * shared, heads)):
                soften(head)
        for head in range(heads):
            mix(head)

        pairs, trades, moves = [], [], []

        def project(c):
            lanes = slice(c * cut, (c + 1) * cut)
            if r == 0:
                out_loads[c][0].wait()
                out_loads[c][1].wait()
            return dot(act_buf, outer[:, lanes]) + dot(a_buf, attn_w[:, lanes])

        def keep(c, share):
            core_part[r, c] = share[half:].astype(BF16)
            mine[:, c * cut : (c + 1) * cut] = share[:half]

        def pair(c):
            pairs.append(send(core_part.at[r, c], core_land.at[r, c],
                              core_send.at[r, c], core_recv.at[r, c], {"sp": partner}))

        def straight(c):
            return r == ROUNDS - 1 and c >= chunks // 2

        def far(c):
            return r < ROUNDS - 1 and c == min(1, chunks - 1)

        def trade(c):
            lanes = slice(c * cut, (c + 1) * cut)
            span = pl.ds(c * cut, cut)
            pairs[c].wait_recv()
            both = mine[:, lanes] + core_land[r, c].astype(F32)
            group = []
            if straight(c):
                for k in reversed(range(chips)):
                    term = factors[r, 2:3, lanes] * both[k * rows : (k + 1) * rows]
                    if k == 0:
                        term = term + gathered[r, 0, 0, :, lanes].astype(F32)
                    chip_part[r, c, k] = term.astype(BF16)
                    group.append(send(chip_part.at[r, c, k], chip_land.at[r, c, (chips - k) % chips],
                                      chip_send.at[r, c, k], chip_recv.at[r, c, k],
                                      {"section": following, "sp": at_chip(k)}))
                trades.append(group)
                return
            if far(c):
                for k in range(chips):
                    term = factors[r, 2:3, lanes] * both[k * rows : (k + 1) * rows]
                    if k == 0:
                        term = term + gathered[r, 0, 0, :, lanes].astype(F32)
                    far_part[r, k] = term.astype(BF16)
                for k in reversed(range(chips)):
                    group.append(send(far_part.at[r], far_land.at[r, (chips - k) % chips],
                                      chip_send.at[r, c, k], chip_recv.at[r, c, k],
                                      {"section": following, "sp": at_chip(k)}))
                trades.append(group)
                return
            mine[:rows, lanes] = both[:rows]
            for k in range(1, chips):
                chip_part[r, c, k] = both[k * rows : (k + 1) * rows].astype(BF16)
                group.append(send(chip_part.at[r, c, k], chip_land.at[r, c, chips - k],
                                  chip_send.at[r, c, k], chip_recv.at[r, c, k], {"sp": at_chip(k)}))
            trades.append(group)

        def finish(c):
            lanes = slice(c * cut, (c + 1) * cut)
            span = pl.ds(c * cut, cut)
            if far(c):
                moves.append(None)
                return
            for copy in trades[c]:
                copy.wait_recv()
            if straight(c):
                summed = chip_land[r, c, 0].astype(F32)
                for k in range(1, chips):
                    summed = summed + chip_land[r, c, k].astype(F32)
                x_out[:, lanes] = summed.astype(BF16)
                return
            summed = mine[:rows, lanes]
            for k in range(1, chips):
                summed = summed + chip_land[r, c, k].astype(F32)
            fresh[r, c] = (
                gathered[r, 0, 0, :, lanes].astype(F32) + factors[r, 2:3, lanes] * summed
            ).astype(BF16)
            group = []
            for k in reversed(range(chips if r < ROUNDS - 1 else 1)):
                target = x_out.at[:, span] if r == ROUNDS - 1 else gathered.at[r + 1, 0, (chips - k) % chips, :, span]
                group.append(send(fresh.at[r, c], target, next_send.at[r, c, k], next_recv.at[r, c, k],
                                  {"section": following, "sp": at_chip(k)}))
            moves.append(group[::-1])

        for c in range(chunks + 4):
            if c < chunks:
                share = project(c)
            if 0 < c <= chunks:
                pair(c - 1)
            if c > 3:
                trade(c - 4)
            if c < chunks:
                keep(c, share)

        if r < ROUNDS - 1:
            for c in range(chunks):
                finish(c)

        for side in range(CORES):
            for k in range(chips):
                owner = lax.rem(chip + k, chips) * CORES + (core if side == 0 else 1 - core)
                there = pl.ds(pl.multiple_of(owner * rows, rows), rows)
                here = slice(side * half + k * rows, side * half + (k + 1) * rows)
                for head in range(heads):
                    lanes = slice(head * HD, (head + 1) * HD)
                    k_new[there, lanes] = keys[head][here]
                v_new[there, :] = made[2][here]
        target = kv if r < ROUNDS - 1 else kv_out
        for which, new in ((0, k_new), (1, v_new)):
            for p in range(blocks):
                there = slice(p * total_rows, (p + 1) * total_rows)
                hit = jnp.broadcast_to(patch, new.shape) == p
                target[which, there, :] = jnp.where(
                    hit, new[...].astype(F32), kv[which, there, :].astype(F32)).astype(BF16)

        if r == ROUNDS - 1:
            for c in range(chunks):
                finish(c)

    for group in moves:
        for copy in group:
            copy.wait_recv()
    for copy in sends:
        copy.wait_send()


def shards(sections, peers, slots, patch_of_slot, step_of_slot, modulation, w_qkv, qk_scale,
           w_mlp_in, w_attn_out, w_mlp_out, kv_cache):
    rows, width = slots.shape[1:]
    local = w_qkv.shape[3]
    hidden = w_mlp_in.shape[2]
    chips = peers // CORES
    half = chips * rows
    total_rows = peers * rows
    cut = divides(width, 512)
    chunks = width // cut
    loads = 2 + 3 + 1 + hidden // divides(hidden, 512) + 2 * chunks
    dma = pltpu.SemaphoreType.DMA
    vmem = pl.BlockSpec(memory_space=pltpu.VMEM)
    anywhere = pl.BlockSpec(memory_space=pl.ANY)
    x, kv = pl.pallas_call(
        functools.partial(kernel, sections, chips),
        out_shape=(
            pltpu.VMEM((rows, width), BF16),
            pltpu.VMEM(kv_cache.shape[1:], BF16),
        ),
        in_specs=[anywhere] * 10,
        out_specs=(vmem, vmem),
        scratch_shapes=[
            pltpu.VMEM((3, width, local), BF16),
            pltpu.VMEM((width, hidden), BF16),
            pltpu.VMEM((local, width), BF16),
            pltpu.VMEM((hidden, width), BF16),
            pltpu.VMEM(kv_cache.shape[1:], BF16),
            pltpu.VMEM((3, modulation.shape[1], width), BF16),
            pltpu.VMEM(qk_scale.shape[1:], BF16),
            pltpu.VMEM((ROUNDS, CORES, chips, rows, width), BF16),
            pltpu.VMEM((half, width), F32),
            pltpu.VMEM((ROUNDS, chunks, half, cut), BF16),
            pltpu.VMEM((ROUNDS, chunks, half, cut), BF16),
            pltpu.VMEM((ROUNDS, chunks, chips, rows, cut), BF16),
            pltpu.VMEM((ROUNDS, chunks, chips, rows, cut), BF16),
            pltpu.VMEM((ROUNDS, chunks, rows, cut), BF16),
            pltpu.VMEM((ROUNDS, chips, rows, cut), BF16),
            pltpu.VMEM((ROUNDS, chips, chips, rows, cut), BF16),
            pltpu.VMEM((padded(total_rows), width), BF16),
            pltpu.VMEM((padded(total_rows), local), BF16),
            pltpu.VMEM((padded(total_rows), hidden), BF16),
            pltpu.VMEM((total_rows, local), BF16),
            pltpu.VMEM((total_rows, local), BF16),
            pltpu.VMEM((ROUNDS, 8, width), F32),
            pltpu.SMEM(patch_of_slot.shape, jnp.int32),
            pltpu.SMEM(step_of_slot.shape, jnp.int32),
            dma((loads,)),
            dma,
            dma((2,)),
            dma((CORES, chips)),
            dma((CORES, chips)),
            dma((ROUNDS, chunks)),
            dma((ROUNDS, chunks)),
            dma((ROUNDS, chunks, chips)),
            dma((ROUNDS, chunks, chips)),
            dma((ROUNDS, chunks, chips)),
            dma((ROUNDS, chunks, chips)),
            dma((ROUNDS, chunks, chips)),
            dma((ROUNDS, chunks, chips)),
        ],
        compiler_params=pltpu.CompilerParams(
            collective_id=0, has_side_effects=True, vmem_limit_bytes=60 * 1024 * 1024
        ),
    )(
        patch_of_slot, step_of_slot, slots[0], jnp.transpose(modulation[0], (1, 0, 2)), qk_scale[0],
        jnp.transpose(w_qkv[0], (1, 0, 2)), w_mlp_in[0], w_attn_out[0], w_mlp_out[0], kv_cache[0],
    )
    return (x[None], kv[None])


def solution(mesh):
    return jax.shard_map(
        functools.partial(shards, mesh.shape["section"], mesh.shape["sp"]),
        mesh=mesh,
        in_specs=(
            P("section", "sp", None),
            P(),
            P(),
            P("section", None, None, None),
            P("section", None, None, "sp"),
            P("section", None, None),
            P("section", None, "sp"),
            P("section", "sp", None),
            P("section", "sp", None),
            P("section", None, None, "sp"),
        ),
        out_specs=(P("section", "sp", None), P("section", None, None, "sp")),
        check_vma=False,
    )
```
